256 devices in a mesh: space: 16 (over x, z_hi), tm: 16 (over y, z_lo, core).
Axes of the slice: x: 4, y: 4, z: 8 (z_hi: 4, z_lo: 2; z = z_hi * 2 + z_lo), core: 2. Of those that a mesh axis runs over, the one named last changes fastest.
Arguments:
- latent: float32 [24, 1024, 2048], P(None, 'space', 'tm'), may hold values from -1.8 to 1.8
- events: int32 [24, 1024, 2048], P(None, 'space', 'tm'), may hold values from 0 to 7
- log_base: float32 [24, 1024, 2048], P(None, 'space', 'tm'), may hold values from -1.5 to 0.5
- innovation: float32 [24, 1024, 2048], P(None, 'space', 'tm'), may hold values from -6 to 6
- kappa_sq: float32 [24, 1024], replicated, may hold values from 0.3 to 3
- chol_factor: float32 [2048, 2048], P(None, 'tm'), as said below
- step_size: float32 [1], replicated, may hold values from 0.02 to 0.08
Outputs:
- gradient: float32 [24, 1024, 2048], P(None, 'space', 'tm')
- proposal: float32 [24, 1024, 2048], P(None, 'space', 'tm')
The draws below stay inside these ranges and needn't reach their ends.
Inputs may be any that keep to these rules, and one draw needn't show every extreme that they name: chol_factor is lower triangular with a positive diagonal.
All inputs are finite; a program needn't handle non-finite values.
Results may differ from the reference program's by a relative error of at most 0.000067.
Values sent between devices are 32-bit elements; how exact they have to be, the bound alone decides.
A program may use at most 64 MiB of HBM per device.

```python
import math
import jax
import jax.numpy as jnp
from jax import lax

R = 24
C = 1024
TT = 2048


def draw_chol_factor(key, part):
    key_diag, key_lower = jax.random.split(key)
    diagonal = jax.random.uniform(key_diag, (TT,), jnp.float32, 0.2, 0.45)
    lower_part = jax.random.normal(key_lower, (TT, TT), jnp.float32) * (0.4 / math.sqrt(TT))
    position = jnp.arange(TT)
    below = jnp.where(position[:, None] > position[None, :], lower_part, 0.0)
    return jnp.where(position[:, None] == position[None, :], diagonal[:, None], below)


def set_ends(result, own_key, smallest, largest):
    extent = result.shape
    place = [jax.random.randint(jax.random.fold_in(own_key, axis), (), 0, extent[axis]) for axis in range(len(extent))]
    result = result.at[tuple(place)].set(smallest)
    longest = extent.index(max(extent))
    place[longest] = (place[longest] + 1) % extent[longest]
    return result.at[tuple(place)].set(largest)


def block_scale(own_key, dims, cuts, low, high):
    gain = 1.0
    for dim, parts in cuts:
        steps = jax.random.uniform(jax.random.fold_in(jax.random.fold_in(own_key, 6), dim), (parts,), jnp.float32, low / len(cuts), high / len(cuts))
        gain = gain * jnp.repeat(jnp.exp(steps), dims[dim] // parts).reshape((-1,) + (1,) * (len(dims) - 1 - dim))
    return gain


def gaussian(key, extent, deviation, bound, shards=(), dtype=jnp.bfloat16):
    result = deviation * jax.random.normal(key, extent, jnp.float32)
    if shards:
        result = result * block_scale(key, extent, shards, -0.22, 0.18)
    return jnp.clip(result, -bound, bound).astype(dtype)


def setup_inputs(seed: int = 0) -> dict:
    streams_of = jax.random.split(jax.random.key(seed), 8)
    return {
        "latent": gaussian(streams_of[0], (R, C, TT), 0.3, 1.8, ((1, 16), (2, 16)), jnp.float32),
        "events": set_ends(jax.random.randint(streams_of[1], (R, C, TT), 0, 8), jax.random.fold_in(streams_of[1], 1), 0, 7).astype(jnp.int32),
        "log_base": jnp.clip(-1.5 + 2.0 * jax.random.uniform(streams_of[2], (R, C, TT), jnp.float32) ** block_scale(streams_of[2], (R, C, TT), ((1, 16), (2, 16)), -0.2, 0.2), -1.5, 0.5),
        "innovation": gaussian(streams_of[3], (R, C, TT), 1.0, 6.0, ((1, 16), (2, 16)), jnp.float32),
        "kappa_sq": jnp.clip(jnp.exp(jax.random.uniform(streams_of[4], (R, C), jnp.float32, math.log(0.3), math.log(3.0))), 0.3, 3.0),
        "chol_factor": draw_chol_factor(jax.random.fold_in(streams_of[7], 71), 0),
        "step_size": jnp.clip(jnp.exp(jax.random.uniform(streams_of[6], (1,), jnp.float32, math.log(0.02), math.log(0.08))), 0.02, 0.08),
    }


def operate(field, kappa_sq):
    padded = jnp.pad(field, ((1, 1), (1, 1), (0, 0)))
    beside = padded[2:, 1:-1] + padded[:-2, 1:-1]
    beside = beside + padded[1:-1, 2:] + padded[1:-1, :-2]
    return (kappa_sq[:, :, None] + 4.0) * field - beside

def reference(latent, events, log_base, innovation, kappa_sq, chol_factor, step_size):
    spatial = operate(operate(latent, kappa_sq), kappa_sq)
    flattened = spatial.reshape(R * C, TT)
    projected = jnp.dot(flattened, chol_factor, precision=lax.Precision.HIGHEST, preferred_element_type=jnp.float32)
    prior_term = jnp.dot(projected, chol_factor.T, precision=lax.Precision.HIGHEST, preferred_element_type=jnp.float32)
    prior_term = prior_term.reshape(R, C, TT)
    gradient = events.astype(jnp.float32) - jnp.exp(log_base + latent) - prior_term
    proposal = latent + step_size[0] * gradient + jnp.sqrt(2.0 * step_size[0]) * innovation
    return (gradient, proposal)
```

```python
import jax
import jax.numpy as jnp
from jax import lax
from jax.sharding import PartitionSpec as P


def halo(block, width):
    count = lax.axis_size("space")
    forward = [(i, i + 1) for i in range(count - 1)]
    backward = [(target, source) for source, target in forward]
    cols = block.shape[1]
    low = lax.ppermute(lax.slice_in_dim(block, cols - width, None, axis=1), "space", forward)
    high = lax.ppermute(lax.slice_in_dim(block, 0, width, axis=1), "space", backward)
    return jnp.concatenate([low, block, high], axis=1)


def operate(extended, kappa_cols):
    centre = extended[:, 1:-1]
    row_padded = jnp.pad(centre, ((1, 1), (0, 0), (0, 0)))
    beside = row_padded[2:] + row_padded[:-2]
    beside = beside + extended[:, 2:] + extended[:, :-2]
    return (kappa_cols[:, :, None] + 4.0) * centre - beside


def gather_factor(chol_cols):
    n = lax.axis_size("tm")
    T, B = chol_cols.shape
    H = (n + 1) * B // 2
    tail = T - H
    j = lax.axis_index("tm")
    pairs = [(i, n - 1 - i) for i in range(n // 2)]
    sent = lax.ppermute(chol_cols[T - tail:], "tm", pairs)
    own_low = lax.dynamic_slice_in_dim(chol_cols, j * B, H, axis=0)
    partner = n - 1 - j
    length = (n - partner) * B - H
    shifted = lax.dynamic_slice_in_dim(
        jnp.concatenate([sent, jnp.zeros((H, B), sent.dtype)], axis=0), tail - length, H, axis=0
    )
    own_tail = chol_cols[T - H:]
    rows = lax.broadcasted_iota(jnp.int32, (H, B), 0)
    own_high = jnp.where(rows < length, shifted, own_tail)
    piece = jnp.where(j < n // 2, own_low, own_high)
    gathered = lax.all_gather(piece, "tm", axis=0, tiled=False)
    blocks = []
    for c in range(n):
        if c < n // 2:
            p = n - 1 - c
            length_c = (n - c) * B - H
            nonzero = jnp.concatenate([gathered[c], gathered[p, :length_c]], axis=0)
        else:
            p = n - 1 - c
            length_p = (n - p) * B - H
            nonzero = gathered[c, length_p:]
        blocks.append(jnp.concatenate([jnp.zeros((c * B, B), nonzero.dtype), nonzero], axis=0))
    return jnp.concatenate(blocks, axis=1)


def local(latent, events, log_base, innovation, kappa_sq, chol_factor, step_size):
    row_count, col_count, time_count = latent.shape
    space_count = lax.axis_size("space")
    col_index = lax.axis_index("space")
    padded_kappa = jnp.pad(kappa_sq, ((0, 0), (1, 1)))
    kappa_wide = lax.dynamic_slice(
        padded_kappa, (jnp.int32(0), col_index * col_count), (row_count, col_count + 2)
    )
    full = gather_factor(chol_factor)
    extended = halo(latent, 2)
    first_pass = operate(extended, kappa_wide)
    cols = lax.broadcasted_iota(jnp.int32, (1, col_count + 2, 1), 1)
    outside = ((cols == 0) & (col_index == 0)) | ((cols == col_count + 1) & (col_index == space_count - 1))
    first_pass = jnp.where(outside, 0.0, first_pass)
    spatial = operate(first_pass, kappa_wide[:, 1:-1])
    cell_count = row_count * col_count
    flattened = spatial.reshape(cell_count, time_count)
    by_cell = lax.all_to_all(flattened, "tm", 0, 1, tiled=True)
    projected = jnp.dot(
        by_cell, full, precision=lax.Precision.HIGHEST, preferred_element_type=jnp.float32
    )
    prior_cells = lax.dot_general(
        projected,
        full,
        (((1,), (1,)), ((), ())),
        precision=lax.Precision.HIGHEST,
        preferred_element_type=jnp.float32,
    )
    prior = lax.all_to_all(prior_cells, "tm", 1, 0, tiled=True)
    prior_term = prior.reshape(row_count, col_count, time_count)
    gradient = events.astype(jnp.float32) - jnp.exp(log_base + latent) - prior_term
    proposal = latent + step_size[0] * gradient + jnp.sqrt(2.0 * step_size[0]) * innovation
    return (gradient, proposal)


def solution(mesh):
    in_specs = (
        P(None, "space", "tm"),
        P(None, "space", "tm"),
        P(None, "space", "tm"),
        P(None, "space", "tm"),
        P(),
        P(None, "tm"),
        P(),
    )
    out_specs = (P(None, "space", "tm"), P(None, "space", "tm"))
    return jax.shard_map(local, mesh=mesh, in_specs=in_specs, out_specs=out_specs, check_vma=False)
```

```python
import jax
import jax.numpy as jnp
from jax import lax
from jax.sharding import Mesh
from jax.sharding import PartitionSpec as P

TM = ("chip", "core")


def halo(block, width):
    count = lax.axis_size("space")
    forward = [(i, i + 1) for i in range(count - 1)]
    backward = [(target, source) for source, target in forward]
    cols = block.shape[1]
    low = lax.ppermute(lax.slice_in_dim(block, cols - width, None, axis=1), "space", forward)
    high = lax.ppermute(lax.slice_in_dim(block, 0, width, axis=1), "space", backward)
    return jnp.concatenate([low, block, high], axis=1)


def operate(extended, kappa_cols):
    centre = extended[:, 1:-1]
    row_padded = jnp.pad(centre, ((1, 1), (0, 0), (0, 0)))
    beside = row_padded[2:] + row_padded[:-2]
    beside = beside + extended[:, 2:] + extended[:, :-2]
    return (kappa_cols[:, :, None] + 4.0) * centre - beside


def gather_factor(chol_cols):
    g = lax.axis_size("chip")
    cores = lax.axis_size("core")
    T, B = chol_cols.shape
    S = cores * B
    H = (2 * T - (g - 1) * S) // 2
    tail = T - H
    k = lax.axis_index("chip")
    pairs = [(i, g - 1 - i) for i in range(g // 2)]
    sent = lax.ppermute(chol_cols[H:], "chip", pairs)
    own_low = lax.dynamic_slice_in_dim(chol_cols, k * S, H, axis=0)
    partner = g - 1 - k
    length = T - partner * S - H
    shifted = lax.dynamic_slice_in_dim(
        jnp.concatenate([sent, jnp.zeros((H, B), sent.dtype)], axis=0), tail - length, H, axis=0
    )
    own_tail = chol_cols[T - H:]
    rows = lax.broadcasted_iota(jnp.int32, (H, B), 0)
    own_high = jnp.where(rows < length, shifted, own_tail)
    piece = jnp.where(k < g // 2, own_low, own_high)
    gathered = lax.all_gather(piece, "chip", axis=0, tiled=False)
    blocks = []
    for c in range(g):
        p = g - 1 - c
        if c < g // 2:
            length_c = T - c * S - H
            nonzero = jnp.concatenate([gathered[c], gathered[p, :length_c]], axis=0)
        else:
            length_p = T - p * S - H
            nonzero = gathered[c, length_p:]
        blocks.append(jnp.concatenate([jnp.zeros((c * S, B), nonzero.dtype), nonzero], axis=0))
    return jnp.stack(blocks, axis=0)


def local(latent, events, log_base, innovation, kappa_sq, chol_factor, step_size):
    row_count, col_count, time_count = latent.shape
    g = lax.axis_size("chip")
    cores = lax.axis_size("core")
    space_count = lax.axis_size("space")
    col_index = lax.axis_index("space")
    padded_kappa = jnp.pad(kappa_sq, ((0, 0), (1, 1)))
    kappa_wide = lax.dynamic_slice(
        padded_kappa, (jnp.int32(0), col_index * col_count), (row_count, col_count + 2)
    )
    factor = gather_factor(chol_factor)
    extended = halo(latent, 2)
    first_pass = operate(extended, kappa_wide)
    cols = lax.broadcasted_iota(jnp.int32, (1, col_count + 2, 1), 1)
    outside = ((cols == 0) & (col_index == 0)) | ((cols == col_count + 1) & (col_index == space_count - 1))
    first_pass = jnp.where(outside, 0.0, first_pass)
    spatial = operate(first_pass, kappa_wide[:, 1:-1])
    cell_count = row_count * col_count
    group = cell_count // g
    flattened = spatial.reshape(cell_count, time_count)
    by_chip = lax.all_to_all(flattened, "chip", 0, 1, tiled=True)
    both = lax.all_gather(by_chip.reshape(group, g, time_count), "core", axis=0, tiled=False)
    hours = jnp.transpose(both, (1, 2, 0, 3)).reshape(group, g * cores * time_count)
    projected = lax.dot_general(
        hours, factor, (((1,), (1,)), ((), ())),
        precision=lax.Precision.HIGHEST, preferred_element_type=jnp.float32,
    )
    partial = lax.dot_general(
        projected, factor, (((1, 2), (0, 2)), ((), ())),
        precision=lax.Precision.HIGHEST, preferred_element_type=jnp.float32,
    )
    split = jnp.transpose(partial.reshape(group, g, cores, time_count), (2, 0, 1, 3))
    summed = lax.psum_scatter(split, "core", scatter_dimension=0, tiled=True)[0]
    prior = lax.all_to_all(summed, "chip", 1, 0, tiled=True)
    prior_term = prior.reshape(row_count, col_count, time_count)
    gradient = events.astype(jnp.float32) - jnp.exp(log_base + latent) - prior_term
    proposal = latent + step_size[0] * gradient + jnp.sqrt(2.0 * step_size[0]) * innovation
    return (gradient, proposal)


def solution(mesh):
    space = mesh.shape["space"]
    tm = mesh.shape["tm"]
    view = Mesh(mesh.devices.reshape(space, tm // 2, 2), ("space", "chip", "core"))
    big = P(None, "space", TM)
    in_specs = (big, big, big, big, P(), P(None, TM), P())
    out_specs = (big, big)
    return jax.shard_map(local, mesh=view, in_specs=in_specs, out_specs=out_specs, check_vma=False)
```

```python
import jax
import jax.numpy as jnp
from jax import lax
from jax.experimental import pallas as pl
from jax.experimental.pallas import tpu as pltpu
from jax.sharding import Mesh
from jax.sharding import PartitionSpec as P

TM = ("chip", "core")
MESH = pl.DeviceIdType.MESH


def halo(block, width):
    count = lax.axis_size("space")
    forward = [(i, i + 1) for i in range(count - 1)]
    backward = [(target, source) for source, target in forward]
    cols = block.shape[1]
    low = lax.ppermute(lax.slice_in_dim(block, cols - width, None, axis=1), "space", forward)
    high = lax.ppermute(lax.slice_in_dim(block, 0, width, axis=1), "space", backward)
    return jnp.concatenate([low, block, high], axis=1)


def operate(extended, kappa_cols):
    centre = extended[:, 1:-1]
    row_padded = jnp.pad(centre, ((1, 1), (0, 0), (0, 0)))
    beside = row_padded[2:] + row_padded[:-2]
    beside = beside + extended[:, 2:] + extended[:, :-2]
    return (kappa_cols[:, :, None] + 4.0) * centre - beside


def gather_kernel(chol_ref, zero, out_ref, send_sems, recv_sems, local_sems):
    G = out_ref.shape[0]
    CH = out_ref.shape[1] // G
    space = lax.axis_index("space")
    core = lax.axis_index("core")
    me = lax.axis_index("chip")
    barrier = pltpu.get_barrier_semaphore()
    for d in range(1, G):
        pl.semaphore_signal(barrier, inc=1, device_id=(space, lax.rem(me + d, G), core), device_id_type=MESH)
    pl.semaphore_wait(barrier, G - 1)

    def chunk(i):
        return pl.ds(pl.multiple_of((me + i) * CH, CH), CH)

    def remote(d, i):
        return pltpu.make_async_remote_copy(
            src_ref=chol_ref.at[chunk(i)],
            dst_ref=out_ref.at[me, chunk(i)],
            send_sem=send_sems.at[d * G + i],
            recv_sem=recv_sems.at[me * G + i],
            device_id=(space, lax.rem(me + d, G), core),
            device_id_type=MESH,
        )

    def own(i):
        return pltpu.make_async_copy(chol_ref.at[chunk(i)], out_ref.at[me, chunk(i)], local_sems.at[i])

    def blank(k, i):
        return pltpu.make_async_copy(zero, out_ref.at[k, pl.ds(i * CH, CH)], local_sems.at[G + k * G + i])

    for i in range(G):
        @pl.when(me + i < G)
        def _():
            for d in range(1, G):
                remote(d, i).start()
    for i in range(G):
        @pl.when(me + i < G)
        def _():
            own(i).start()
    for k in range(G):
        for i in range(k):
            blank(k, i).start()
    for k in range(G):
        for i in range(k):
            blank(k, i).wait()
    for i in range(G):
        @pl.when(me + i < G)
        def _():
            own(i).wait()
            for d in range(1, G):
                remote(d, i).wait_send()
    for k in range(G):
        for i in range(G - k):
            @pl.when(me != k)
            def _():
                rows = pl.ds((k + i) * CH, CH)
                pltpu.make_async_remote_copy(
                    src_ref=chol_ref.at[rows],
                    dst_ref=out_ref.at[k, rows],
                    send_sem=send_sems.at[i],
                    recv_sem=recv_sems.at[k * G + i],
                    device_id=(space, k, core),
                    device_id_type=MESH,
                ).wait_recv()


def gather_factor(chol_cols):
    G = lax.axis_size("chip")
    T, B = chol_cols.shape
    CH = T // G
    return pl.pallas_call(
        gather_kernel,
        out_shape=jax.ShapeDtypeStruct((G, T, B), chol_cols.dtype),
        in_specs=[pl.BlockSpec(memory_space=pl.ANY)] * 2,
        out_specs=pl.BlockSpec(memory_space=pl.ANY),
        scratch_shapes=[
            pltpu.SemaphoreType.DMA((G * G,)),
            pltpu.SemaphoreType.DMA((G * G,)),
            pltpu.SemaphoreType.DMA((G + G * G,)),
        ],
        compiler_params=pltpu.CompilerParams(collective_id=0, has_side_effects=True),
    )(chol_cols, jnp.zeros((CH, B), chol_cols.dtype))


def local(latent, events, log_base, innovation, kappa_sq, chol_factor, step_size):
    row_count, col_count, time_count = latent.shape
    g = lax.axis_size("chip")
    cores = lax.axis_size("core")
    space_count = lax.axis_size("space")
    col_index = lax.axis_index("space")
    padded_kappa = jnp.pad(kappa_sq, ((0, 0), (1, 1)))
    kappa_wide = lax.dynamic_slice(
        padded_kappa, (jnp.int32(0), col_index * col_count), (row_count, col_count + 2)
    )
    factor = gather_factor(chol_factor)
    extended = halo(latent, 2)
    first_pass = operate(extended, kappa_wide)
    cols = lax.broadcasted_iota(jnp.int32, (1, col_count + 2, 1), 1)
    outside = ((cols == 0) & (col_index == 0)) | ((cols == col_count + 1) & (col_index == space_count - 1))
    first_pass = jnp.where(outside, 0.0, first_pass)
    spatial = operate(first_pass, kappa_wide[:, 1:-1])
    cell_count = row_count * col_count
    group = cell_count // g
    flattened = spatial.reshape(cell_count, time_count)
    by_chip = lax.all_to_all(flattened, "chip", 0, 1, tiled=True)
    both = lax.all_gather(by_chip.reshape(group, g, time_count), "core", axis=0, tiled=False)
    hours = jnp.transpose(both, (1, 2, 0, 3)).reshape(group, g * cores * time_count)
    projected = lax.dot_general(
        hours, factor, (((1,), (1,)), ((), ())),
        precision=lax.Precision.HIGHEST, preferred_element_type=jnp.float32,
    )
    partial = lax.dot_general(
        projected, factor, (((1, 2), (0, 2)), ((), ())),
        precision=lax.Precision.HIGHEST, preferred_element_type=jnp.float32,
    )
    split = jnp.transpose(partial.reshape(group, g, cores, time_count), (2, 0, 1, 3))
    summed = lax.psum_scatter(split, "core", scatter_dimension=0, tiled=True)[0]
    prior = lax.all_to_all(summed, "chip", 1, 0, tiled=True)
    prior_term = prior.reshape(row_count, col_count, time_count)
    gradient = events.astype(jnp.float32) - jnp.exp(log_base + latent) - prior_term
    proposal = latent + step_size[0] * gradient + jnp.sqrt(2.0 * step_size[0]) * innovation
    return (gradient, proposal)


def solution(mesh):
    space = mesh.shape["space"]
    tm = mesh.shape["tm"]
    view = Mesh(mesh.devices.reshape(space, tm // 2, 2), ("space", "chip", "core"))
    big = P(None, "space", TM)
    in_specs = (big, big, big, big, P(), P(None, TM), P())
    out_specs = (big, big)
    return jax.shard_map(local, mesh=view, in_specs=in_specs, out_specs=out_specs, check_vma=False)
```

```python
import jax
import jax.numpy as jnp
from jax import lax
from jax.experimental import pallas as pl
from jax.experimental.pallas import tpu as pltpu
from jax.sharding import PartitionSpec as P


def halo(block, width):
    count = lax.axis_size("space")
    forward = [(i, i + 1) for i in range(count - 1)]
    backward = [(target, source) for source, target in forward]
    cols = block.shape[1]
    low = lax.ppermute(lax.slice_in_dim(block, cols - width, None, axis=1), "space", forward)
    high = lax.ppermute(lax.slice_in_dim(block, 0, width, axis=1), "space", backward)
    return jnp.concatenate([low, block, high], axis=1)


def operate(extended, kappa_cols):
    centre = extended[:, 1:-1]
    row_padded = jnp.pad(centre, ((1, 1), (0, 0), (0, 0)))
    beside = row_padded[2:] + row_padded[:-2]
    beside = beside + extended[:, 2:] + extended[:, :-2]
    return (kappa_cols[:, :, None] + 4.0) * centre - beside


def fold_rows(T, B, n):
    return -(-(T + B) // (2 * B)) * B


def gather_factor(chol_cols):
    n = lax.axis_size("tm")
    T, B = chol_cols.shape
    H = fold_rows(T, B, n)
    tail = T - H
    j = lax.axis_index("tm")
    pairs = [(i, n - 1 - i) for i in range(n // 2)]
    sent = lax.ppermute(chol_cols[T - tail:], "tm", pairs)
    own_low = lax.dynamic_slice_in_dim(chol_cols, j * B, H, axis=0)
    partner = n - 1 - j
    length = (n - partner) * B - H
    shifted = lax.dynamic_slice_in_dim(
        jnp.concatenate([sent, jnp.zeros((H, B), sent.dtype)], axis=0), tail - length, H, axis=0
    )
    own_tail = chol_cols[T - H:]
    rows = lax.broadcasted_iota(jnp.int32, (H, B), 0)
    own_high = jnp.where(rows < length, shifted, own_tail)
    piece = jnp.where(j < n // 2, own_low, own_high)
    return lax.all_gather(piece, "tm", axis=0, tiled=False)


def segments(n, T, B, H):
    out = []
    for c in range(n):
        p = n - 1 - c
        if c < n // 2:
            segs = [(c, 0, c * B, H)]
            if T - c * B - H > 0:
                segs.append((p, 0, c * B + H, T - c * B - H))
        else:
            segs = [(c, H - (T - c * B), c * B, T - c * B)]
        out.append(segs)
    return out


def prior_kernel(s_ref, g_ref, out_ref):
    n, H, B = g_ref.shape
    N, T = s_ref.shape
    out_ref[...] = jnp.zeros_like(out_ref)
    for segs in segments(n, T, B, H):
        proj = None
        for slot, r0, h0, count in segs:
            term = jnp.dot(
                s_ref[:, h0:h0 + count], g_ref[slot, r0:r0 + count, :],
                precision=lax.Precision.HIGHEST, preferred_element_type=jnp.float32,
            )
            proj = term if proj is None else proj + term
        for slot, r0, h0, count in segs:
            out_ref[:, h0:h0 + count] += lax.dot_general(
                proj, g_ref[slot, r0:r0 + count, :], (((1,), (1,)), ((), ())),
                precision=lax.Precision.HIGHEST, preferred_element_type=jnp.float32,
            )


def prior_of(by_cell, gathered):
    n, H, B = gathered.shape
    N, T = by_cell.shape
    flops = 0
    for segs in segments(n, T, B, H):
        flops += sum(4 * N * count * B for _, _, _, count in segs)
    return pl.pallas_call(
        prior_kernel,
        out_shape=jax.ShapeDtypeStruct((N, T), jnp.float32),
        in_specs=[pl.BlockSpec(memory_space=pltpu.VMEM)] * 2,
        out_specs=pl.BlockSpec(memory_space=pltpu.VMEM),
        cost_estimate=pl.CostEstimate(
            flops=flops, transcendentals=0, bytes_accessed=4 * (2 * N * T + n * H * B)
        ),
    )(by_cell, gathered)


def local(latent, events, log_base, innovation, kappa_sq, chol_factor, step_size):
    row_count, col_count, time_count = latent.shape
    space_count = lax.axis_size("space")
    col_index = lax.axis_index("space")
    padded_kappa = jnp.pad(kappa_sq, ((0, 0), (1, 1)))
    kappa_wide = lax.dynamic_slice(
        padded_kappa, (jnp.int32(0), col_index * col_count), (row_count, col_count + 2)
    )
    gathered = gather_factor(chol_factor)
    extended = halo(latent, 2)
    first_pass = operate(extended, kappa_wide)
    cols = lax.broadcasted_iota(jnp.int32, (1, col_count + 2, 1), 1)
    outside = ((cols == 0) & (col_index == 0)) | ((cols == col_count + 1) & (col_index == space_count - 1))
    first_pass = jnp.where(outside, 0.0, first_pass)
    spatial = operate(first_pass, kappa_wide[:, 1:-1])
    cell_count = row_count * col_count
    flattened = spatial.reshape(cell_count, time_count)
    by_cell = lax.all_to_all(flattened, "tm", 0, 1, tiled=True)
    prior_cells = prior_of(by_cell, gathered)
    prior = lax.all_to_all(prior_cells, "tm", 1, 0, tiled=True)
    prior_term = prior.reshape(row_count, col_count, time_count)
    gradient = events.astype(jnp.float32) - jnp.exp(log_base + latent) - prior_term
    proposal = latent + step_size[0] * gradient + jnp.sqrt(2.0 * step_size[0]) * innovation
    return (gradient, proposal)


def solution(mesh):
    in_specs = (
        P(None, "space", "tm"),
        P(None, "space", "tm"),
        P(None, "space", "tm"),
        P(None, "space", "tm"),
        P(),
        P(None, "tm"),
        P(),
    )
    out_specs = (P(None, "space", "tm"), P(None, "space", "tm"))
    return jax.shard_map(local, mesh=mesh, in_specs=in_specs, out_specs=out_specs, check_vma=False)
```

```python
import jax
import jax.numpy as jnp
from jax import lax
from jax.experimental import pallas as pl
from jax.experimental.pallas import tpu as pltpu
from jax.sharding import PartitionSpec as P


def halo(block, width):
    count = lax.axis_size("space")
    forward = [(i, i + 1) for i in range(count - 1)]
    backward = [(target, source) for source, target in forward]
    cols = block.shape[1]
    low = lax.ppermute(lax.slice_in_dim(block, cols - width, None, axis=1), "space", forward)
    high = lax.ppermute(lax.slice_in_dim(block, 0, width, axis=1), "space", backward)
    return jnp.concatenate([low, block, high], axis=1)


def operate(extended, kappa_cols):
    centre = extended[:, 1:-1]
    row_padded = jnp.pad(centre, ((1, 1), (0, 0), (0, 0)))
    beside = row_padded[2:] + row_padded[:-2]
    beside = beside + extended[:, 2:] + extended[:, :-2]
    return (kappa_cols[:, :, None] + 4.0) * centre - beside


def fold_rows(T, B, n):
    return -(-(T + B) // (2 * B)) * B


def gather_factor(chol_cols):
    n = lax.axis_size("tm")
    T, B = chol_cols.shape
    H = fold_rows(T, B, n)
    tail = T - H
    j = lax.axis_index("tm")
    pairs = [(i, n - 1 - i) for i in range(n // 2)]
    sent = lax.ppermute(chol_cols[T - tail:], "tm", pairs)
    own_low = lax.dynamic_slice_in_dim(chol_cols, j * B, H, axis=0)
    partner = n - 1 - j
    length = (n - partner) * B - H
    shifted = lax.dynamic_slice_in_dim(
        jnp.concatenate([sent, jnp.zeros((H, B), sent.dtype)], axis=0), tail - length, H, axis=0
    )
    own_tail = chol_cols[T - H:]
    rows = lax.broadcasted_iota(jnp.int32, (H, B), 0)
    own_high = jnp.where(rows < length, shifted, own_tail)
    piece = jnp.where(j < n // 2, own_low, own_high)
    return lax.all_gather(piece, "tm", axis=0, tiled=False)


def segments(n, T, B, H):
    out = []
    for c in range(n):
        p = n - 1 - c
        if c < n // 2:
            segs = [(c, 0, c * B, H)]
            if T - c * B - H > 0:
                segs.append((p, 0, c * B + H, T - c * B - H))
        else:
            segs = [(c, H - (T - c * B), c * B, T - c * B)]
        out.append(segs)
    return out


def prior_kernel(s_ref, g_ref, out_ref):
    n, H, B = g_ref.shape
    N, T = s_ref.shape
    out_ref[...] = jnp.zeros_like(out_ref)
    for segs in segments(n, T, B, H):
        proj = None
        for slot, r0, h0, count in segs:
            term = jnp.dot(
                s_ref[:, h0:h0 + count], g_ref[slot, r0:r0 + count, :],
                precision=lax.Precision.HIGH, preferred_element_type=jnp.float32,
            )
            proj = term if proj is None else proj + term
        for slot, r0, h0, count in segs:
            out_ref[:, h0:h0 + count] += lax.dot_general(
                proj, g_ref[slot, r0:r0 + count, :], (((1,), (1,)), ((), ())),
                precision=lax.Precision.HIGH, preferred_element_type=jnp.float32,
            )


def prior_of(by_cell, gathered):
    n, H, B = gathered.shape
    N, T = by_cell.shape
    flops = 0
    for segs in segments(n, T, B, H):
        flops += sum(4 * N * count * B for _, _, _, count in segs)
    return pl.pallas_call(
        prior_kernel,
        out_shape=jax.ShapeDtypeStruct((N, T), jnp.float32),
        in_specs=[pl.BlockSpec(memory_space=pltpu.VMEM)] * 2,
        out_specs=pl.BlockSpec(memory_space=pltpu.VMEM),
        cost_estimate=pl.CostEstimate(
            flops=flops, transcendentals=0, bytes_accessed=4 * (2 * N * T + n * H * B)
        ),
    )(by_cell, gathered)


def local(latent, events, log_base, innovation, kappa_sq, chol_factor, step_size):
    row_count, col_count, time_count = latent.shape
    space_count = lax.axis_size("space")
    col_index = lax.axis_index("space")
    padded_kappa = jnp.pad(kappa_sq, ((0, 0), (1, 1)))
    kappa_wide = lax.dynamic_slice(
        padded_kappa, (jnp.int32(0), col_index * col_count), (row_count, col_count + 2)
    )
    gathered = gather_factor(chol_factor)
    extended = halo(latent, 2)
    first_pass = operate(extended, kappa_wide)
    cols = lax.broadcasted_iota(jnp.int32, (1, col_count + 2, 1), 1)
    outside = ((cols == 0) & (col_index == 0)) | ((cols == col_count + 1) & (col_index == space_count - 1))
    first_pass = jnp.where(outside, 0.0, first_pass)
    spatial = operate(first_pass, kappa_wide[:, 1:-1])
    cell_count = row_count * col_count
    flattened = spatial.reshape(cell_count, time_count)
    by_cell = lax.all_to_all(flattened, "tm", 0, 1, tiled=True)
    prior_cells = prior_of(by_cell, gathered)
    prior = lax.all_to_all(prior_cells, "tm", 1, 0, tiled=True)
    prior_term = prior.reshape(row_count, col_count, time_count)
    gradient = events.astype(jnp.float32) - jnp.exp(log_base + latent) - prior_term
    proposal = latent + step_size[0] * gradient + jnp.sqrt(2.0 * step_size[0]) * innovation
    return (gradient, proposal)


def solution(mesh):
    in_specs = (
        P(None, "space", "tm"),
        P(None, "space", "tm"),
        P(None, "space", "tm"),
        P(None, "space", "tm"),
        P(),
        P(None, "tm"),
        P(),
    )
    out_specs = (P(None, "space", "tm"), P(None, "space", "tm"))
    return jax.shard_map(local, mesh=mesh, in_specs=in_specs, out_specs=out_specs, check_vma=False)
```
